32 devices in a mesh: dp: 16 (over z, y, x), tensor: 2 (over core).
Axes of the slice: x: 2, y: 2, z: 4, core: 2. Of those that a mesh axis runs over, the one named last changes fastest.
Arguments:
- inputs: bfloat16 [25088, 512], P(('dp', 'tensor')), may hold values from -6 to 6
- cotangent: bfloat16 [25088, 512], P(('dp', 'tensor')), may hold values from -6 to 6
- region_ids: int32 [196], replicated, may hold values from 0 to 3
- rel_index: int32 [49, 49], replicated, may hold values from 0 to 168
- norm1_gain: bfloat16 [2, 512], replicated, may hold values from 0.5 to 1.5
- norm1_bias: bfloat16 [2, 512], replicated, may hold values from -1.75 to 1.75
- w_qkv: bfloat16 [2, 3, 512, 512], P(None, None, 'dp', 'tensor'), may hold values from -0.25 to 0.25
- qv_bias: bfloat16 [2, 2, 512], P(None, None, 'tensor'), may hold values from -1.75 to 1.75
- bias_table: bfloat16 [2, 16, 169], P(None, 'tensor'), may hold values from -3 to 250
- w_proj: bfloat16 [2, 512, 512], P(None, 'tensor', 'dp'), may hold values from -0.75 to 0.75
- proj_bias: bfloat16 [2, 512], replicated, may hold values from -1.75 to 1.75
- norm2_gain: bfloat16 [2, 512], replicated, may hold values from 0.5 to 1.5
- norm2_bias: bfloat16 [2, 512], replicated, may hold values from -1.75 to 1.75
- w_fc1: bfloat16 [2, 512, 2048], P(None, 'dp', 'tensor'), may hold values from -0.25 to 0.25
- fc1_bias: bfloat16 [2, 2048], P(None, 'tensor'), may hold values from -3 to 3
- w_fc2: bfloat16 [2, 2048, 512], P(None, 'tensor', 'dp'), may hold values from -0.125 to 0.125
- fc2_bias: bfloat16 [2, 512], replicated, may hold values from -1.75 to 1.75
Outputs:
- outputs: float32 [25088, 512], P(('dp', 'tensor'))
- input_grad: float32 [25088, 512], P(('dp', 'tensor'))
- norm1_gain_grad: float32 [2, 512], replicated
- norm1_bias_grad: float32 [2, 512], replicated
- w_qkv_grad: float32 [2, 3, 512, 512], P(None, None, 'dp', 'tensor')
- qv_bias_grad: float32 [2, 2, 512], P(None, None, 'tensor')
- bias_table_grad: float32 [2, 16, 169], P(None, 'tensor')
- w_proj_grad: float32 [2, 512, 512], P(None, 'tensor', 'dp')
- proj_bias_grad: float32 [2, 512], replicated
- norm2_gain_grad: float32 [2, 512], replicated
- norm2_bias_grad: float32 [2, 512], replicated
- w_fc1_grad: float32 [2, 512, 2048], P(None, 'dp', 'tensor')
- fc1_bias_grad: float32 [2, 2048], P(None, 'tensor')
- w_fc2_grad: float32 [2, 2048, 512], P(None, 'tensor', 'dp')
- fc2_bias_grad: float32 [2, 512], replicated
The draws below stay inside these ranges and needn't reach their ends.
All inputs are finite; a program needn't handle non-finite values.
Results may differ from the reference program's by a relative error of at most 0.025.
Values may be sent and summed in bfloat16 or wider, within the bound.
A program may use at most 192 MiB of HBM per device.

```python
import jax
import jax.numpy as jnp
from jax import lax

C = 512
HEADS = 16
HD = 32
FF = 2048
GRID = 14
WIN = 7
SHIFT = 3
LAYERS = 2
IMG_DEV = 8
TABLE = 169
IMAGES = 128
TOKENS = 25088
N_DP = 16


def draw_bias_table(key, part):
    base_key = jax.random.fold_in(key, 0)
    shape = (LAYERS, HEADS, TABLE)
    values = jnp.clip(jax.random.normal(base_key, shape, jnp.float32), -3.0, 3.0)
    return values.astype(jnp.bfloat16)


def place_ends(values, rng, least, high):
    dims = values.shape
    place = [jax.random.randint(jax.random.fold_in(rng, axis), (), 0, dims[axis]) for axis in range(len(dims))]
    values = values.at[tuple(place)].set(least)
    longest = dims.index(max(dims))
    place[longest] = (place[longest] + 1) % dims[longest]
    return values.at[tuple(place)].set(high)


def levels(own_key, extent, cuts, least, largest):
    def one(dim, parts):
        steps = jax.random.uniform(jax.random.fold_in(jax.random.fold_in(own_key, 6), dim), (parts,), jnp.float32, least / len(cuts), largest / len(cuts))
        return jnp.repeat(jnp.exp(steps), extent[dim] // parts).reshape((-1,) + (1,) * (len(extent) - dim - 1))

    gain = one(*cuts[0])
    for cut in cuts[1:]:
        gain = gain * one(*cut)
    return gain


def normal_values(rng, extent, scale, bound, shards=(), held_as=jnp.bfloat16):
    factor_of = levels(rng, extent, shards, -0.22, 0.18) if shards else 1.0
    entries = jax.random.normal(rng, extent, jnp.float32) * scale * factor_of
    return jnp.minimum(jnp.maximum(entries, -bound), bound).astype(held_as)


def setup_inputs(seed: int = 0) -> dict:
    arg_keys = jax.random.split(jax.random.key(seed), 18)
    inputs = normal_values(arg_keys[0], (TOKENS, C), 1.0, 6.0, ((0, 32),))
    cotangent = normal_values(arg_keys[1], (TOKENS, C), 1.0, 6.0, ((0, 32),))
    region_ids = place_ends(jax.random.randint(arg_keys[2], (GRID * GRID,), 0, 4), jax.random.fold_in(arg_keys[2], 1), 0, 3).astype(jnp.int32)
    rel_index = place_ends(jax.random.randint(arg_keys[3], (WIN * WIN, WIN * WIN), 0, TABLE), jax.random.fold_in(arg_keys[3], 1), 0, TABLE - 1).astype(jnp.int32)
    norm1_gain = jnp.clip(1.0 + 0.1 * jax.random.normal(arg_keys[4], (LAYERS, C), jnp.float32), 0.5, 1.5).astype(jnp.bfloat16)
    norm1_bias = normal_values(arg_keys[5], (LAYERS, C), 0.3, 1.75)
    w_qkv = normal_values(arg_keys[6], (LAYERS, 3, C, C), C ** -0.5, 0.25, ((2, 16), (3, 2)))
    qv_bias = normal_values(arg_keys[7], (LAYERS, 2, C), 0.3, 1.75, ((2, 2),))
    bias_table = draw_bias_table(jax.random.fold_in(arg_keys[17], 71), 0)
    w_proj = normal_values(arg_keys[9], (LAYERS, C, C), (C // WIN) ** -0.5, 0.75, ((1, 2), (2, 16)))
    proj_bias = normal_values(arg_keys[10], (LAYERS, C), 0.3, 1.75)
    norm2_gain = jnp.clip(1.0 + 0.1 * jax.random.normal(arg_keys[11], (LAYERS, C), jnp.float32), 0.5, 1.5).astype(jnp.bfloat16)
    norm2_bias = normal_values(arg_keys[12], (LAYERS, C), 0.3, 1.75)
    w_fc1 = normal_values(arg_keys[13], (LAYERS, C, FF), C ** -0.5, 0.25, ((1, 16), (2, 2)))
    fc1_bias = normal_values(arg_keys[14], (LAYERS, FF), 0.5, 3.0, ((1, 2),))
    w_fc2 = normal_values(arg_keys[15], (LAYERS, FF, C), FF ** -0.5, 0.125, ((1, 2), (2, 16)))
    fc2_bias = normal_values(arg_keys[16], (LAYERS, C), 0.3, 1.75)
    return dict(inputs=inputs, cotangent=cotangent, region_ids=region_ids, rel_index=rel_index, norm1_gain=norm1_gain, norm1_bias=norm1_bias, w_qkv=w_qkv, qv_bias=qv_bias, bias_table=bias_table, w_proj=w_proj, proj_bias=proj_bias, norm2_gain=norm2_gain, norm2_bias=norm2_bias, w_fc1=w_fc1, fc1_bias=fc1_bias, w_fc2=w_fc2, fc2_bias=fc2_bias)


EPS = 1e-05
MASKED = -100.0
EXACT_PRECISION = lax.Precision.HIGHEST

def to_grid(tokens, images):
    per_side = GRID // WIN
    shaped = tokens.reshape(images, per_side, per_side, WIN, WIN, -1)
    return shaped.transpose(0, 1, 3, 2, 4, 5).reshape(images, GRID, GRID, -1)

def to_windows(grid_rows, images):
    per_side = GRID // WIN
    shaped = grid_rows.reshape(images, per_side, WIN, per_side, WIN, -1)
    return shaped.transpose(0, 1, 3, 2, 4, 5).reshape(images * GRID * GRID, -1)

def rolled(tokens, images, offset):
    return to_windows(jnp.roll(to_grid(tokens, images), offset, axis=(1, 2)), images)

def normalize(residual):
    average = lax.optimization_barrier(jnp.mean(residual, -1, keepdims=True))
    centered = residual - average
    inverse = lax.rsqrt(lax.optimization_barrier(jnp.mean(centered * centered, -1, keepdims=True)) + EPS)
    return (centered * inverse, inverse)

def norm_back(grad_out, normed, inverse, gain_value):
    scaled = grad_out * gain_value
    return inverse * (scaled - lax.optimization_barrier(jnp.mean(scaled, -1, keepdims=True)) - normed * lax.optimization_barrier(jnp.mean(scaled * normed, -1, keepdims=True)))

def gelu_parts(hidden_pre):
    cumulative = 0.5 * (1.0 + lax.erf(hidden_pre * 0.7071067811865476))
    density = jnp.exp(-0.5 * hidden_pre * hidden_pre) * 0.3989422804014327
    return (hidden_pre * cumulative, cumulative + hidden_pre * density)

def product(first_operand, second_operand):
    return jnp.dot(first_operand, second_operand, preferred_element_type=jnp.float32)

def exact_einsum(pattern, first_operand, second_operand):
    return jnp.einsum(pattern, first_operand.astype(jnp.float32), second_operand.astype(jnp.float32), precision=EXACT_PRECISION)

def reference(inputs, cotangent, region_ids, rel_index, norm1_gain, norm1_bias, w_qkv, qv_bias, bias_table, w_proj, proj_bias, norm2_gain, norm2_bias, w_fc1, fc1_bias, w_fc2, fc2_bias):
    per_side = GRID // WIN
    windows = per_side * per_side
    win_tokens = WIN * WIN
    score_scale = HD ** (-0.5)
    one_hot = (rel_index[:, :, None] == jnp.arange(TABLE, dtype=jnp.int32)[None, None, :]).astype(jnp.float32)
    regions = region_ids.reshape(windows, win_tokens)
    shift_mask = jnp.where(regions[:, :, None] == regions[:, None, :], 0.0, MASKED).astype(jnp.float32)
    mask_list = [jnp.zeros_like(shift_mask), shift_mask]
    rel_biases = [exact_einsum('ijm,hm->hij', one_hot, bias_table[layer_index]) for layer_index in range(LAYERS)]
    group = IMG_DEV * 4 if N_DP % 4 == 0 else IMG_DEV
    blocks = IMAGES // group
    block_rows = group * GRID * GRID
    head_shape = (group, windows, win_tokens, HEADS, HD)

    def scores_of(layer_index, queries, key_rows):
        return exact_einsum('bwihd,bwjhd->bwhij', queries, key_rows) + rel_biases[layer_index][None, None] + mask_list[layer_index % 2][None, :, None]

    def layer_forward(layer_index, residual):
        shifted_layer = layer_index % 2 == 1
        normed_attn, inverse_attn = normalize(residual)
        attn_in = (normed_attn * norm1_gain[layer_index].astype(jnp.float32) + norm1_bias[layer_index].astype(jnp.float32)).astype(jnp.bfloat16)
        if shifted_layer:
            attn_in = rolled(attn_in, group, -SHIFT)
        stacked_qkv = w_qkv[layer_index]
        query_pre = product(attn_in, stacked_qkv[0]) + qv_bias[layer_index, 0].astype(jnp.float32)
        queries = (query_pre * score_scale).astype(jnp.bfloat16).reshape(head_shape)
        key_rows = product(attn_in, stacked_qkv[1]).astype(jnp.bfloat16).reshape(head_shape)
        values = (product(attn_in, stacked_qkv[2]) + qv_bias[layer_index, 1].astype(jnp.float32)).astype(jnp.bfloat16).reshape(head_shape)
        scores = scores_of(layer_index, queries, key_rows)
        highest = lax.optimization_barrier(jnp.max(scores, -1, keepdims=True))
        exponent = jnp.exp(scores - highest)
        denominator = lax.optimization_barrier(jnp.sum(exponent, -1, keepdims=True))
        attention = exponent / denominator
        log_total = highest + jnp.log(denominator)
        mixture = exact_einsum('bwhij,bwjhd->bwihd', attention.astype(jnp.bfloat16), values).astype(jnp.bfloat16).reshape(block_rows, C)
        projected = product(mixture, w_proj[layer_index])
        if shifted_layer:
            projected = rolled(projected, group, SHIFT)
        residual_mid = residual + projected + proj_bias[layer_index].astype(jnp.float32)
        normed_ffn, inverse_ffn = normalize(residual_mid)
        ffn_in = (normed_ffn * norm2_gain[layer_index].astype(jnp.float32) + norm2_bias[layer_index].astype(jnp.float32)).astype(jnp.bfloat16)
        hidden_pre = product(ffn_in, w_fc1[layer_index]) + fc1_bias[layer_index].astype(jnp.float32)
        activated, gelu_slope = gelu_parts(hidden_pre)
        hidden = activated.astype(jnp.bfloat16)
        residual_out = residual_mid + product(hidden, w_fc2[layer_index]) + fc2_bias[layer_index].astype(jnp.float32)
        stored = (normed_attn, inverse_attn, attn_in, queries, key_rows, values, log_total, mixture, normed_ffn, inverse_ffn, ffn_in, gelu_slope, hidden)
        return (residual_out, stored)

    def layer_backward(layer_index, stored, grad_out):
        shifted_layer = layer_index % 2 == 1
        normed_attn, inverse_attn, attn_in, queries, key_rows, values, log_total, mixture, normed_ffn, inverse_ffn, ffn_in, gelu_slope, hidden = stored
        grad_fc2_bias = lax.optimization_barrier(jnp.sum(grad_out, 0))
        grad_low = grad_out.astype(jnp.bfloat16)
        grad_hidden = product(grad_low, w_fc2[layer_index].T)
        grad_w_fc2 = product(hidden.T, grad_low)
        grad_pre = grad_hidden * gelu_slope
        grad_pre_low = grad_pre.astype(jnp.bfloat16)
        grad_fc1_bias = lax.optimization_barrier(jnp.sum(grad_pre, 0))
        grad_w_fc1 = product(ffn_in.T, grad_pre_low)
        grad_ffn_in = product(grad_pre_low, w_fc1[layer_index].T)
        grad_norm2_gain = lax.optimization_barrier(jnp.sum(grad_ffn_in * normed_ffn, 0))
        grad_norm2_bias = lax.optimization_barrier(jnp.sum(grad_ffn_in, 0))
        grad_mid = grad_out + norm_back(grad_ffn_in, normed_ffn, inverse_ffn, norm2_gain[layer_index].astype(jnp.float32))
        grad_proj_bias = lax.optimization_barrier(jnp.sum(grad_mid, 0))
        grad_mid_low = grad_mid.astype(jnp.bfloat16)
        if shifted_layer:
            grad_mid_low = rolled(grad_mid_low, group, -SHIFT)
        grad_mixture = product(grad_mid_low, w_proj[layer_index].T)
        grad_w_proj = product(mixture.T, grad_mid_low)
        grad_mixture_low = grad_mixture.astype(jnp.bfloat16).reshape(head_shape)
        scores = scores_of(layer_index, queries, key_rows)
        attention = jnp.exp(scores - log_total)
        attention_low = attention.astype(jnp.bfloat16)
        grad_values = exact_einsum('bwhij,bwihd->bwjhd', attention_low, grad_mixture_low).reshape(block_rows, C)
        grad_attention = exact_einsum('bwihd,bwjhd->bwhij', grad_mixture_low, values)
        row_inner = lax.optimization_barrier(jnp.sum(attention * grad_attention, -1, keepdims=True))
        grad_scores = attention * (grad_attention - row_inner)
        grad_table = exact_einsum('ijm,hij->hm', one_hot, lax.optimization_barrier(jnp.sum(grad_scores, (0, 1))))
        grad_scores_low = grad_scores.astype(jnp.bfloat16)
        grad_queries = exact_einsum('bwhij,bwjhd->bwihd', grad_scores_low, key_rows).reshape(block_rows, C) * score_scale
        grad_keys = exact_einsum('bwhij,bwihd->bwjhd', grad_scores_low, queries).reshape(block_rows, C)
        grad_qv_bias = jnp.stack([lax.optimization_barrier(jnp.sum(grad_queries, 0)), lax.optimization_barrier(jnp.sum(grad_values, 0))])
        grad_parts = [grad_queries.astype(jnp.bfloat16), grad_keys.astype(jnp.bfloat16), grad_values.astype(jnp.bfloat16)]
        stacked_qkv = w_qkv[layer_index]
        grad_attn_in = product(grad_parts[0], stacked_qkv[0].T) + product(grad_parts[1], stacked_qkv[1].T) + product(grad_parts[2], stacked_qkv[2].T)
        grad_w_qkv = jnp.stack([product(attn_in.T, grad_part) for grad_part in grad_parts])
        if shifted_layer:
            grad_attn_in = rolled(grad_attn_in, group, SHIFT)
        grad_norm1_gain = lax.optimization_barrier(jnp.sum(grad_attn_in * normed_attn, 0))
        grad_norm1_bias = lax.optimization_barrier(jnp.sum(grad_attn_in, 0))
        grad_in = grad_mid + norm_back(grad_attn_in, normed_attn, inverse_attn, norm1_gain[layer_index].astype(jnp.float32))
        return (grad_in, (grad_norm1_gain, grad_norm1_bias, grad_w_qkv, grad_qv_bias, grad_table, grad_w_proj, grad_proj_bias, grad_norm2_gain, grad_norm2_bias, grad_w_fc1, grad_fc1_bias, grad_w_fc2, grad_fc2_bias))

    def one_block(running_grads, pieces):
        block_in, block_cot = pieces
        residual = block_in.astype(jnp.float32)
        forward_store = []
        for layer_index in range(LAYERS):
            residual, stored = layer_forward(layer_index, residual)
            forward_store.append(stored)
        grad_residual = block_cot.astype(jnp.float32)
        layer_grads = [None] * LAYERS
        for layer_index in reversed(range(LAYERS)):
            grad_residual, layer_grads[layer_index] = layer_backward(layer_index, forward_store[layer_index], grad_residual)
        stacked = tuple((jnp.stack([layer_grads[layer_index][position] for layer_index in range(LAYERS)]) for position in range(13)))
        return (tuple((running + addend for running, addend in zip(running_grads, stacked))), (residual, grad_residual))
    params = (norm1_gain, norm1_bias, w_qkv, qv_bias, bias_table, w_proj, proj_bias, norm2_gain, norm2_bias, w_fc1, fc1_bias, w_fc2, fc2_bias)
    zero_grads = tuple((jnp.zeros(param.shape, jnp.float32) for param in params))
    totals, (block_outs, block_grads) = lax.scan(one_block, zero_grads, (inputs.reshape(blocks, block_rows, C), cotangent.reshape(blocks, block_rows, C)))
    return (block_outs.reshape(TOKENS, C), block_grads.reshape(TOKENS, C), totals[0], totals[1], totals[2], totals[3], totals[4], totals[5], totals[6], totals[7], totals[8], totals[9], totals[10], totals[11], totals[12])
```

```python
import functools

import jax
import jax.numpy as jnp
from jax import lax
from jax.experimental import pallas as pl
from jax.experimental.pallas import tpu as pltpu
from jax.sharding import PartitionSpec as P

HD = 32
GRID = 14
WIN = 7
SHIFT = 3
LAYERS = 2
TABLE = 169
EPS = 1e-05
MASKED = -100.0
PADDED = -1e30
SLOT = 64
LANES = 128
EXACT_PRECISION = lax.Precision.HIGHEST
F32 = jnp.float32
BF16 = jnp.bfloat16


def normalize(residual):
    average = jnp.mean(residual, -1, keepdims=True)
    centered = residual - average
    inverse = lax.rsqrt(jnp.mean(centered * centered, -1, keepdims=True) + EPS)
    return (centered * inverse, inverse)


def norm_back(grad_out, normed, inverse, gain_value):
    scaled = grad_out * gain_value
    return inverse * (
        scaled
        - jnp.mean(scaled, -1, keepdims=True)
        - normed * jnp.mean(scaled * normed, -1, keepdims=True)
    )


def gelu_parts(hidden_pre):
    cumulative = 0.5 * (1.0 + lax.erf(hidden_pre * 0.7071067811865476))
    density = jnp.exp(-0.5 * hidden_pre * hidden_pre) * 0.3989422804014327
    return (hidden_pre * cumulative, cumulative + hidden_pre * density)


def dot(a, b, ca=1, cb=0):
    return lax.dot_general(a, b, (((ca,), (cb,)), ((), ())), preferred_element_type=F32)


def stack_heads(block, masks):
    return jnp.concatenate([block * m for m in masks], axis=0)


def merge_heads(stacked, masks):
    total = None
    for h, m in enumerate(masks):
        part = stacked[h * SLOT : (h + 1) * SLOT] * m
        total = part if total is None else total + part
    return total


def head_masks(dtype):
    lane = lax.broadcasted_iota(jnp.int32, (SLOT, LANES), 1)
    return [
        jnp.where((lane >= h * HD) & (lane < (h + 1) * HD), 1.0, 0.0).astype(dtype)
        for h in range(LANES // HD)
    ]


def probabilities(queries_stacked, keys, bias):
    scores = dot(queries_stacked, keys, 1, 1) + bias
    exponent = jnp.exp(scores - jnp.max(scores, -1, keepdims=True))
    return exponent / jnp.sum(exponent, -1, keepdims=True)


def attention_kernel(qkv_ref, bias_ref, mask_ref, out_ref):
    width = out_ref.shape[1]
    low, full = head_masks(BF16), head_masks(F32)
    mask = jnp.concatenate([mask_ref[0]] * len(low), axis=0)
    for g in range(width // LANES):
        q = qkv_ref[:, g * LANES : (g + 1) * LANES]
        k = qkv_ref[:, width + g * LANES : width + (g + 1) * LANES]
        v = qkv_ref[:, 2 * width + g * LANES : 2 * width + (g + 1) * LANES]
        attention = probabilities(stack_heads(q, low), k, bias_ref[g] + mask)
        mixed = dot(attention.astype(BF16), v)
        out_ref[:, g * LANES : (g + 1) * LANES] = merge_heads(mixed, full).astype(BF16)


def attention_back_kernel(scale, qkv_ref, dmix_ref, bias_ref, mask_ref, dqkv_ref, dscore_ref, dbias_ref):
    width = dmix_ref.shape[1]
    low, full = head_masks(BF16), head_masks(F32)
    mask = jnp.concatenate([mask_ref[0]] * len(low), axis=0)

    @pl.when(pl.program_id(0) == 0)
    def _():
        dscore_ref[...] = jnp.zeros_like(dscore_ref)
        dbias_ref[...] = jnp.zeros_like(dbias_ref)

    def put(part, g, value):
        at = slice(part * width + g * LANES, part * width + (g + 1) * LANES)
        dqkv_ref[:, at] = value.astype(BF16)
        if part != 1:
            rows = value[0:8]
            for r in range(1, SLOT // 8):
                rows = rows + value[r * 8 : (r + 1) * 8]
            dbias_ref[:, at] += rows

    for g in range(width // LANES):
        q = qkv_ref[:, g * LANES : (g + 1) * LANES]
        k = qkv_ref[:, width + g * LANES : width + (g + 1) * LANES]
        v = qkv_ref[:, 2 * width + g * LANES : 2 * width + (g + 1) * LANES]
        dm = dmix_ref[:, g * LANES : (g + 1) * LANES]
        q_stacked = stack_heads(q, low)
        dm_stacked = stack_heads(dm, low)
        attention = probabilities(q_stacked, k, bias_ref[g] + mask)
        dattention = dot(dm_stacked, v, 1, 1)
        inner = jnp.sum(attention * dattention, -1, keepdims=True)
        dscores = attention * (dattention - inner)
        dscore_ref[g] += dscores
        dl = dscores.astype(BF16)
        put(0, g, merge_heads(dot(dl, k), full) * scale)
        put(1, g, dot(dl, q_stacked, 0, 0))
        put(2, g, dot(attention.astype(BF16), dm_stacked, 0, 0))


def attention_forward(qkv, bias, mask):
    rows, width = qkv.shape[0], qkv.shape[1] // 3
    windows = mask.shape[0]
    return pl.pallas_call(
        attention_kernel,
        grid=(rows // SLOT,),
        out_shape=jax.ShapeDtypeStruct((rows, width), BF16),
        in_specs=[
            pl.BlockSpec((SLOT, 3 * width), lambda i: (i, 0)),
            pl.BlockSpec(bias.shape, lambda i: (0, 0, 0)),
            pl.BlockSpec((1, SLOT, SLOT), lambda i: (lax.rem(i, windows), 0, 0)),
        ],
        out_specs=pl.BlockSpec((SLOT, width), lambda i: (i, 0)),
        cost_estimate=pl.CostEstimate(
            flops=rows * width * SLOT * 16, bytes_accessed=rows * width * 8, transcendentals=rows * width * 2
        ),
        name="attention_forward",
    )(qkv, bias, mask)


def attention_backward(qkv, dmix, bias, mask, scale):
    rows, width = dmix.shape
    windows = mask.shape[0]
    return pl.pallas_call(
        functools.partial(attention_back_kernel, scale),
        grid=(rows // SLOT,),
        out_shape=(
            jax.ShapeDtypeStruct((rows, 3 * width), BF16),
            jax.ShapeDtypeStruct(bias.shape, F32),
            jax.ShapeDtypeStruct((8, 3 * width), F32),
        ),
        in_specs=[
            pl.BlockSpec((SLOT, 3 * width), lambda i: (i, 0)),
            pl.BlockSpec((SLOT, width), lambda i: (i, 0)),
            pl.BlockSpec(bias.shape, lambda i: (0, 0, 0)),
            pl.BlockSpec((1, SLOT, SLOT), lambda i: (lax.rem(i, windows), 0, 0)),
        ],
        out_specs=(
            pl.BlockSpec((SLOT, 3 * width), lambda i: (i, 0)),
            pl.BlockSpec(bias.shape, lambda i: (0, 0, 0)),
            pl.BlockSpec((8, 3 * width), lambda i: (0, 0)),
        ),
        cost_estimate=pl.CostEstimate(
            flops=rows * width * SLOT * 40, bytes_accessed=rows * width * 16, transcendentals=rows * width * 2
        ),
        name="attention_backward",
    )(qkv, dmix, bias, mask)


def placement(tokens, shift):
    per_side = GRID // WIN
    slots = tokens // (WIN * WIN) * SLOT
    row = lax.broadcasted_iota(jnp.int32, (slots, tokens), 0)
    column = lax.broadcasted_iota(jnp.int32, (slots, tokens), 1)
    window, p = row // SLOT, row % SLOT
    image, w = window // (per_side * per_side), window % (per_side * per_side)
    gi = (w // per_side * WIN + p // WIN + shift) % GRID
    gj = (w % per_side * WIN + p % WIN + shift) % GRID
    source = (
        image * (GRID * GRID)
        + (gi // WIN * per_side + gj // WIN) * (WIN * WIN)
        + gi % WIN * WIN
        + gj % WIN
    )
    return ((column == source) & (p < WIN * WIN)).astype(BF16)


def pack_weights(w_qkv, w_proj, w_fc1, w_fc2):
    rows = w_qkv.shape[1]
    return jnp.concatenate(
        [w_qkv.transpose(1, 0, 2).reshape(rows, -1), w_proj.T, w_fc1, w_fc2.T], axis=1
    )


def per_device(
    inputs,
    cotangent,
    region_ids,
    rel_index,
    norm1_gain,
    norm1_bias,
    w_qkv,
    qv_bias,
    bias_table,
    w_proj,
    proj_bias,
    norm2_gain,
    norm2_bias,
    w_fc1,
    fc1_bias,
    w_fc2,
    fc2_bias,
):
    n_dp, n_t = lax.axis_size("dp"), lax.axis_size("tensor")
    t_index = lax.axis_index("tensor")
    tokens, width = inputs.shape
    ff_local = fc1_bias.shape[1]
    heads_local = bias_table.shape[1]
    heads = heads_local * n_t
    local = heads_local * HD
    shard = width // n_dp
    cuts = (3 * local, 4 * local, 4 * local + ff_local, 4 * local + 2 * ff_local)
    per_side = GRID // WIN
    windows = per_side * per_side
    win_tokens = WIN * WIN
    score_scale = HD ** (-0.5)
    groups = width // LANES

    def pack_grads(g_qkv, g_proj, g_fc1, g_fc2):
        pieces = []
        for g, n in ((g_qkv, 3), (g_proj, 1), (g_fc1, 1), (g_fc2, 1)):
            shaped = g.astype(BF16).reshape(n_dp, shard, n, n_t, -1)
            pieces.append(shaped.transpose(0, 3, 1, 2, 4).reshape(n_dp, n_t, shard, -1))
        return jnp.concatenate(pieces, -1)

    small = jnp.concatenate([qv_bias.reshape(-1), fc1_bias.reshape(-1), bias_table.reshape(-1)])
    extra = -(-small.shape[0] // (shard * LANES)) * LANES
    small_packed = jnp.pad(small, (0, shard * extra - small.shape[0])).reshape(shard, extra)

    def gather_layer(l):
        packed = pack_weights(w_qkv[l], w_proj[l], w_fc1[l], w_fc2[l])
        if l == 0:
            packed = jnp.concatenate([packed, small_packed], axis=1)
        whole = gather_shards(packed)
        parts = []
        lo = 0
        for n, hi in zip((3, 1, 1, 1), cuts):
            piece = whole[..., lo:hi].reshape(n_dp, n_t, shard, n, (hi - lo) // n)
            parts.append(piece.transpose(0, 2, 3, 1, 4).reshape(width, -1))
            lo = hi
        return parts, whole[0, :, :, lo:].reshape(n_t, -1)

    gathered = [gather_layer(l) for l in range(LAYERS)]
    weights = [parts for parts, _ in gathered]
    small = gathered[0][1][:, : small.shape[0]]
    n_qv, n_fc = qv_bias.size, fc1_bias.size
    qv_full = small[:, :n_qv].reshape(n_t, LAYERS, 2, local).transpose(1, 2, 0, 3).reshape(LAYERS, 2, width)
    fc1_full = small[:, n_qv : n_qv + n_fc].reshape(n_t, LAYERS, ff_local).transpose(1, 0, 2).reshape(LAYERS, -1)
    table_full = (
        small[:, n_qv + n_fc :].reshape(n_t, LAYERS, heads_local, TABLE).transpose(1, 0, 2, 3).reshape(LAYERS, heads, TABLE)
    ).astype(F32)
    fc1_full = fc1_full.astype(F32)
    qv_full = qv_full.astype(F32)

    pad = SLOT - win_tokens
    index_padded = jnp.pad(rel_index, ((0, pad), (0, pad)), constant_values=-1).reshape(-1)
    one_hot = (index_padded[None, :] == jnp.arange(TABLE, dtype=jnp.int32)[:, None]).astype(F32)
    regions = region_ids.reshape(windows, win_tokens)
    shift_mask = jnp.where(regions[:, :, None] == regions[:, None, :], 0.0, MASKED).astype(F32)

    def padded_mask(mask):
        return jnp.pad(
            jnp.pad(mask, ((0, 0), (0, pad), (0, 0))), ((0, 0), (0, 0), (0, pad)), constant_values=PADDED
        )

    masks = [padded_mask(jnp.zeros_like(shift_mask)), padded_mask(shift_mask)]
    biases = [
        jnp.dot(table_full[l], one_hot, precision=EXACT_PRECISION).reshape(groups, LANES // HD * SLOT, SLOT)
        for l in range(LAYERS)
    ]
    places = [placement(tokens, SHIFT * (l % 2)) for l in range(LAYERS)]
    scale_row = jnp.concatenate([jnp.full((width,), score_scale, F32), jnp.ones((2 * width,), F32)])

    residual = inputs.astype(F32)
    store = []
    for l in range(LAYERS):
        qkv_w, proj_w, fc1_w, fc2_w = weights[l]
        place = places[l]
        normed1, inverse1 = normalize(residual)
        attn_in = (normed1 * norm1_gain[l].astype(F32) + norm1_bias[l].astype(F32)).astype(BF16)
        attn_pad = dot(place, attn_in).astype(BF16)
        qkv_bias = jnp.concatenate([qv_full[l, 0], jnp.zeros((width,), F32), qv_full[l, 1]])
        qkv = ((dot(attn_pad, qkv_w) + qkv_bias) * scale_row).astype(BF16)
        mixture = dot(place, attention_forward(qkv, biases[l], masks[l % 2]), 0, 0).astype(BF16)
        residual_mid = residual + dot(mixture, proj_w, 1, 1) + proj_bias[l].astype(F32)
        normed2, inverse2 = normalize(residual_mid)
        ffn_in = (normed2 * norm2_gain[l].astype(F32) + norm2_bias[l].astype(F32)).astype(BF16)
        activated, slope = gelu_parts(dot(ffn_in, fc1_w) + fc1_full[l])
        hidden = activated.astype(BF16)
        slope = slope.astype(BF16)
        store.append((normed1, inverse1, attn_in, qkv, mixture, normed2, inverse2, ffn_in, slope, hidden))
        residual = residual_mid + dot(hidden, fc2_w, 1, 1) + fc2_bias[l].astype(F32)

    g = cotangent.astype(F32)
    weight_grads = [None] * LAYERS
    small_grads = [None] * LAYERS
    for l in reversed(range(LAYERS)):
        qkv_w, proj_w, fc1_w, fc2_w = weights[l]
        place = places[l]
        normed1, inverse1, attn_in, qkv, mixture, normed2, inverse2, ffn_in, slope, hidden = store[l]
        g_fc2_bias = jnp.sum(g, 0)
        gl = g.astype(BF16)
        dpre = dot(gl, fc2_w) * slope.astype(F32)
        dpl = dpre.astype(BF16)
        g_fc1_bias = jnp.sum(dpre, 0)
        g_fc2 = dot(gl, hidden, 0, 0)
        g_fc1 = dot(ffn_in, dpl, 0, 0)
        dffn = dot(dpl, fc1_w, 1, 1)
        g_n2_gain = jnp.sum(dffn * normed2, 0)
        g_n2_bias = jnp.sum(dffn, 0)
        g_mid = g + norm_back(dffn, normed2, inverse2, norm2_gain[l].astype(F32))
        g_proj_bias = jnp.sum(g_mid, 0)
        gm = g_mid.astype(BF16)
        g_proj = dot(gm, mixture, 0, 0)
        dmix = dot(gm, proj_w).astype(BF16)
        dmix_pad = dot(place, dmix).astype(BF16)
        dqkv_pad, dscores, dbias = attention_backward(qkv, dmix_pad, biases[l], masks[l % 2], score_scale)
        g_table = lax.dot_general(
            dscores.reshape(heads, SLOT * SLOT), one_hot, (((1,), (1,)), ((), ())), precision=EXACT_PRECISION
        )
        dqkv = dot(place, dqkv_pad, 0, 0).astype(BF16)
        g_qkv = dot(attn_in, dqkv, 0, 0)
        dattn = dot(dqkv, qkv_w, 1, 1)
        g_n1_gain = jnp.sum(dattn * normed1, 0)
        g_n1_bias = jnp.sum(dattn, 0)
        g = g_mid + norm_back(dattn, normed1, inverse1, norm1_gain[l].astype(F32))
        dbias_rows = jnp.sum(dbias, 0)
        weight_grads[l] = reduce_shards(pack_grads(g_qkv, g_proj, g_fc1, g_fc2)).astype(F32)
        small_grads[l] = [
            g_n1_gain, g_n1_bias, g_proj_bias, g_n2_gain, g_n2_bias, g_fc2_bias,
            dbias_rows[:width], dbias_rows[2 * width :], g_fc1_bias, g_table.reshape(-1),
        ]

    flat = jnp.concatenate([v for l in range(LAYERS) for v in small_grads[l]])
    total = sum_everywhere(flat).reshape(LAYERS, -1)
    vectors = total[:, : 6 * width].reshape(LAYERS, 6, width)
    at = 6 * width
    qv_total = total[:, at : at + 2 * width].reshape(LAYERS, 2, width)
    qv_total = lax.dynamic_slice_in_dim(qv_total, t_index * local, local, 2)
    at += 2 * width
    fc1_total = lax.dynamic_slice_in_dim(total[:, at : at + ff_local * n_t], t_index * ff_local, ff_local, 1)
    at += ff_local * n_t
    table_total = lax.dynamic_slice_in_dim(
        total[:, at:].reshape(LAYERS, heads, TABLE), t_index * heads_local, heads_local, 1
    )
    grads = jnp.stack(weight_grads)
    qkv_total = grads[..., : cuts[0]].reshape(LAYERS, shard, 3, local).transpose(0, 2, 1, 3)
    proj_w_total = grads[..., cuts[0] : cuts[1]].transpose(0, 2, 1)
    fc1_w_total = grads[..., cuts[1] : cuts[2]]
    fc2_w_total = grads[..., cuts[2] :].transpose(0, 2, 1)
    return (
        residual,
        g,
        vectors[:, 0],
        vectors[:, 1],
        qkv_total,
        qv_total,
        table_total,
        proj_w_total,
        vectors[:, 2],
        vectors[:, 3],
        vectors[:, 4],
        fc1_w_total,
        fc1_total,
        fc2_w_total,
        vectors[:, 5],
    )


def gather_shards(packed):
    n_dp, n_t = lax.axis_size("dp"), lax.axis_size("tensor")
    rows = lax.all_gather(packed, ("dp", "tensor"), axis=0, tiled=False)
    return rows.reshape((n_dp, n_t) + packed.shape)


def reduce_shards(packed):
    rows = packed.reshape((-1,) + packed.shape[2:])
    return lax.psum_scatter(rows, ("dp", "tensor"), scatter_dimension=0, tiled=False)


def partners():
    found = []
    for axis in ("tensor", "dp"):
        size, bit = lax.axis_size(axis), 1
        assert size & (size - 1) == 0
        me = lax.axis_index(axis)
        while bit < size:
            found.append((axis, me + bit - 2 * bit * ((me // bit) % 2)))
            bit *= 2
    return found


def exchange_kernel(x_ref, out_ref, held, arrived, send_sem, recv_sem):
    steps = partners()
    barrier = pltpu.get_barrier_semaphore()
    for axis, place in steps:
        pl.semaphore_signal(barrier, inc=1, device_id={axis: place}, device_id_type=pl.DeviceIdType.MESH)
    pl.semaphore_wait(barrier, len(steps))
    for s, (axis, place) in enumerate(steps):
        source = x_ref if s == 0 else held.at[s - 1]
        copy = pltpu.make_async_remote_copy(
            src_ref=source,
            dst_ref=arrived.at[s],
            send_sem=send_sem.at[s],
            recv_sem=recv_sem.at[s],
            device_id={axis: place},
            device_id_type=pl.DeviceIdType.MESH,
        )
        copy.start()
        copy.wait()
        total = source[...] + arrived[s]
        if s < len(steps) - 1:
            held[s] = total
        else:
            out_ref[...] = total


def sum_everywhere(flat):
    size = flat.shape[0]
    rows = -(-size // (8 * LANES)) * 8
    x = jnp.pad(flat, (0, rows * LANES - size)).reshape(rows, LANES)
    n = len(partners())
    total = pl.pallas_call(
        exchange_kernel,
        out_shape=jax.ShapeDtypeStruct(x.shape, F32),
        in_specs=[pl.BlockSpec(memory_space=pltpu.VMEM)],
        out_specs=pl.BlockSpec(memory_space=pltpu.VMEM),
        scratch_shapes=[
            pltpu.VMEM((n,) + x.shape, F32),
            pltpu.VMEM((n,) + x.shape, F32),
            pltpu.SemaphoreType.DMA((n,)),
            pltpu.SemaphoreType.DMA((n,)),
        ],
        compiler_params=pltpu.CompilerParams(collective_id=0, has_side_effects=True),
        name="sum_everywhere",
    )(x)
    return total.reshape(-1)[:size]


def solution(mesh):
    in_specs = (
        P(("dp", "tensor"), None),
        P(("dp", "tensor"), None),
        P(),
        P(),
        P(),
        P(),
        P(None, None, "dp", "tensor"),
        P(None, None, "tensor"),
        P(None, "tensor", None),
        P(None, "tensor", "dp"),
        P(),
        P(),
        P(),
        P(None, "dp", "tensor"),
        P(None, "tensor"),
        P(None, "tensor", "dp"),
        P(),
    )
    out_specs = (
        P(("dp", "tensor"), None),
        P(("dp", "tensor"), None),
        P(),
        P(),
        P(None, None, "dp", "tensor"),
        P(None, None, "tensor"),
        P(None, "tensor", None),
        P(None, "tensor", "dp"),
        P(),
        P(),
        P(),
        P(None, "dp", "tensor"),
        P(None, "tensor"),
        P(None, "tensor", "dp"),
        P(),
    )
    return jax.shard_map(
        per_device, mesh=mesh, in_specs=in_specs, out_specs=out_specs, check_vma=False
    )
```

```python
import functools
import itertools

import jax
import jax.numpy as jnp
from jax import lax
from jax.experimental import pallas as pl
from jax.experimental.pallas import tpu as pltpu
from jax.sharding import PartitionSpec as P

HD = 32
GRID = 14
WIN = 7
SHIFT = 3
LAYERS = 2
TABLE = 169
EPS = 1e-05
MASKED = -100.0
PADDED = -1e30
SLOT = 64
PER_STEP = 2
LANES = 128
EXACT_PRECISION = lax.Precision.HIGHEST
F32 = jnp.float32
BF16 = jnp.bfloat16


def normalize(residual):
    average = jnp.mean(residual, -1, keepdims=True)
    centered = residual - average
    inverse = lax.rsqrt(jnp.mean(centered * centered, -1, keepdims=True) + EPS)
    return (centered * inverse, inverse)


def norm_back(grad_out, normed, inverse, gain_value):
    scaled = grad_out * gain_value
    return inverse * (
        scaled
        - jnp.mean(scaled, -1, keepdims=True)
        - normed * jnp.mean(scaled * normed, -1, keepdims=True)
    )


def gelu_parts(hidden_pre):
    cumulative = 0.5 * (1.0 + lax.erf(hidden_pre * 0.7071067811865476))
    density = jnp.exp(-0.5 * hidden_pre * hidden_pre) * 0.3989422804014327
    return (hidden_pre * cumulative, cumulative + hidden_pre * density)


def dot(a, b, ca=1, cb=0):
    return lax.dot_general(a, b, (((ca,), (cb,)), ((), ())), preferred_element_type=F32)


def stack_heads(block, masks):
    return jnp.concatenate([block * m for m in masks], axis=0)


def merge_heads(stacked, masks):
    total = None
    for h, m in enumerate(masks):
        part = stacked[h * SLOT : (h + 1) * SLOT] * m
        total = part if total is None else total + part
    return total


def head_masks(dtype):
    lane = lax.broadcasted_iota(jnp.int32, (SLOT, LANES), 1)
    return [
        jnp.where((lane >= h * HD) & (lane < (h + 1) * HD), 1.0, 0.0).astype(dtype)
        for h in range(LANES // HD)
    ]


def probabilities(queries_stacked, keys, bias):
    scores = dot(queries_stacked, keys, 1, 1) + bias
    exponent = jnp.exp(scores - jnp.max(scores, -1, keepdims=True))
    return exponent * (1.0 / jnp.sum(exponent, -1, keepdims=True))


def attention_kernel(qkv_ref, bias_ref, mask_ref, out_ref):
    width = out_ref.shape[1]
    low, full = head_masks(BF16), head_masks(F32)
    for g, w in itertools.product(range(width // LANES), range(mask_ref.shape[0])):
        rows = slice(w * SLOT, (w + 1) * SLOT)
        mask = jnp.concatenate([mask_ref[w]] * len(low), axis=0)
        q = qkv_ref[rows, g * LANES : (g + 1) * LANES]
        k = qkv_ref[rows, width + g * LANES : width + (g + 1) * LANES]
        v = qkv_ref[rows, 2 * width + g * LANES : 2 * width + (g + 1) * LANES]
        attention = probabilities(stack_heads(q, low), k, bias_ref[g] + mask)
        mixed = dot(attention.astype(BF16), v)
        out_ref[rows, g * LANES : (g + 1) * LANES] = merge_heads(mixed, full).astype(BF16)


def attention_back_kernel(scale, qkv_ref, dmix_ref, bias_ref, mask_ref, dqkv_ref, dscore_ref, dbias_ref):
    width = dmix_ref.shape[1]
    low, full = head_masks(BF16), head_masks(F32)

    @pl.when(pl.program_id(0) == 0)
    def _():
        dscore_ref[...] = jnp.zeros_like(dscore_ref)
        dbias_ref[...] = jnp.zeros_like(dbias_ref)

    def put(part, g, at_rows, value):
        at = slice(part * width + g * LANES, part * width + (g + 1) * LANES)
        dqkv_ref[at_rows, at] = value.astype(BF16)
        if part != 1:
            rows = value[0:8]
            for r in range(1, SLOT // 8):
                rows = rows + value[r * 8 : (r + 1) * 8]
            dbias_ref[:, at] += rows

    for g, w in itertools.product(range(width // LANES), range(mask_ref.shape[0])):
        rows = slice(w * SLOT, (w + 1) * SLOT)
        mask = jnp.concatenate([mask_ref[w]] * len(low), axis=0)
        q = qkv_ref[rows, g * LANES : (g + 1) * LANES]
        k = qkv_ref[rows, width + g * LANES : width + (g + 1) * LANES]
        v = qkv_ref[rows, 2 * width + g * LANES : 2 * width + (g + 1) * LANES]
        dm = dmix_ref[rows, g * LANES : (g + 1) * LANES]
        q_stacked = stack_heads(q, low)
        dm_stacked = stack_heads(dm, low)
        attention = probabilities(q_stacked, k, bias_ref[g] + mask)
        dattention = dot(dm_stacked, v, 1, 1)
        inner = jnp.sum(attention * dattention, -1, keepdims=True)
        dscores = attention * (dattention - inner)
        dscore_ref[g] += dscores
        dl = dscores.astype(BF16)
        put(0, g, rows, merge_heads(dot(dl, k), full) * scale)
        put(1, g, rows, dot(dl, q_stacked, 0, 0))
        put(2, g, rows, dot(attention.astype(BF16), dm_stacked, 0, 0))


def attention_forward(qkv, bias, mask):
    rows, width = qkv.shape[0], qkv.shape[1] // 3
    windows = mask.shape[0]
    return pl.pallas_call(
        attention_kernel,
        grid=(rows // (PER_STEP * SLOT),),
        out_shape=jax.ShapeDtypeStruct((rows, width), BF16),
        in_specs=[
            pl.BlockSpec((PER_STEP * SLOT, 3 * width), lambda i: (i, 0)),
            pl.BlockSpec(bias.shape, lambda i: (0, 0, 0)),
            pl.BlockSpec((PER_STEP, SLOT, SLOT), lambda i: (lax.rem(i, windows // PER_STEP), 0, 0)),
        ],
        out_specs=pl.BlockSpec((PER_STEP * SLOT, width), lambda i: (i, 0)),
        cost_estimate=pl.CostEstimate(
            flops=rows * width * SLOT * 16, bytes_accessed=rows * width * 8, transcendentals=rows * width * 2
        ),
        name="attention_forward",
    )(qkv, bias, mask)


def attention_backward(qkv, dmix, bias, mask, scale):
    rows, width = dmix.shape
    windows = mask.shape[0]
    return pl.pallas_call(
        functools.partial(attention_back_kernel, scale),
        grid=(rows // (PER_STEP * SLOT),),
        out_shape=(
            jax.ShapeDtypeStruct((rows, 3 * width), BF16),
            jax.ShapeDtypeStruct(bias.shape, F32),
            jax.ShapeDtypeStruct((8, 3 * width), F32),
        ),
        in_specs=[
            pl.BlockSpec((PER_STEP * SLOT, 3 * width), lambda i: (i, 0)),
            pl.BlockSpec((PER_STEP * SLOT, width), lambda i: (i, 0)),
            pl.BlockSpec(bias.shape, lambda i: (0, 0, 0)),
            pl.BlockSpec((PER_STEP, SLOT, SLOT), lambda i: (lax.rem(i, windows // PER_STEP), 0, 0)),
        ],
        out_specs=(
            pl.BlockSpec((PER_STEP * SLOT, 3 * width), lambda i: (i, 0)),
            pl.BlockSpec(bias.shape, lambda i: (0, 0, 0)),
            pl.BlockSpec((8, 3 * width), lambda i: (0, 0)),
        ),
        cost_estimate=pl.CostEstimate(
            flops=rows * width * SLOT * 40, bytes_accessed=rows * width * 16, transcendentals=rows * width * 2
        ),
        name="attention_backward",
    )(qkv, dmix, bias, mask)


def placement(tokens, shift):
    per_side = GRID // WIN
    slots = tokens // (WIN * WIN) * SLOT
    row = lax.broadcasted_iota(jnp.int32, (slots, tokens), 0)
    column = lax.broadcasted_iota(jnp.int32, (slots, tokens), 1)
    window, p = row // SLOT, row % SLOT
    image, w = window // (per_side * per_side), window % (per_side * per_side)
    gi = (w // per_side * WIN + p // WIN + shift) % GRID
    gj = (w % per_side * WIN + p % WIN + shift) % GRID
    source = (
        image * (GRID * GRID)
        + (gi // WIN * per_side + gj // WIN) * (WIN * WIN)
        + gi % WIN * WIN
        + gj % WIN
    )
    return ((column == source) & (p < WIN * WIN)).astype(BF16)


def pack_weights(w_qkv, w_proj, w_fc1, w_fc2):
    rows = w_qkv.shape[1]
    return jnp.concatenate(
        [w_qkv.transpose(1, 0, 2).reshape(rows, -1), w_proj.T, w_fc1, w_fc2.T], axis=1
    )


def per_device(
    inputs,
    cotangent,
    region_ids,
    rel_index,
    norm1_gain,
    norm1_bias,
    w_qkv,
    qv_bias,
    bias_table,
    w_proj,
    proj_bias,
    norm2_gain,
    norm2_bias,
    w_fc1,
    fc1_bias,
    w_fc2,
    fc2_bias,
):
    n_dp, n_t = lax.axis_size("dp"), lax.axis_size("tensor")
    t_index = lax.axis_index("tensor")
    tokens, width = inputs.shape
    ff_local = fc1_bias.shape[1]
    heads_local = bias_table.shape[1]
    heads = heads_local * n_t
    local = heads_local * HD
    shard = width // n_dp
    cuts = (3 * local, 4 * local, 4 * local + ff_local, 4 * local + 2 * ff_local)
    per_side = GRID // WIN
    windows = per_side * per_side
    win_tokens = WIN * WIN
    score_scale = HD ** (-0.5)
    groups = width // LANES

    def pack_grads(g_qkv, g_proj, g_fc1, g_fc2):
        sides = []
        for t in range(n_t):
            pieces = []
            for g, n in ((g_qkv, 3), (g_proj, 1), (g_fc1, 1), (g_fc2, 1)):
                step = g.shape[1] // (n * n_t)
                pieces += [g[:, (m * n_t + t) * step : (m * n_t + t + 1) * step].astype(BF16) for m in range(n)]
            sides.append(jnp.concatenate(pieces, axis=1).reshape(n_dp, shard, -1))
        return jnp.stack(sides, axis=1)

    small = jnp.concatenate([qv_bias.reshape(-1), fc1_bias.reshape(-1), bias_table.reshape(-1)])
    extra = -(-small.shape[0] // (shard * LANES)) * LANES
    small_packed = jnp.pad(small, (0, shard * extra - small.shape[0])).reshape(shard, extra)

    def gather_layer(l):
        packed = pack_weights(w_qkv[l], w_proj[l], w_fc1[l], w_fc2[l])
        if l == 0:
            packed = jnp.concatenate([packed, small_packed], axis=1)
        whole = gather_shards(packed)
        return whole, whole[0, :, :, cuts[3] :].reshape(n_t, -1)

    def unpack_weights(whole):
        blocks = [whole[:, t].reshape(width, -1) for t in range(n_t)]
        parts = []
        lo = 0
        for n, hi in zip((3, 1, 1, 1), cuts):
            step = (hi - lo) // n
            parts.append(
                jnp.concatenate([b[:, lo + m * step : lo + (m + 1) * step] for m in range(n) for b in blocks], axis=1)
            )
            lo = hi
        return parts

    gathered = [gather_layer(l) for l in range(LAYERS)]
    wholes = [whole for whole, _ in gathered]
    weights = [None] * LAYERS
    small = gathered[0][1][:, : small.shape[0]]
    n_qv, n_fc = qv_bias.size, fc1_bias.size
    qv_full = small[:, :n_qv].reshape(n_t, LAYERS, 2, local).transpose(1, 2, 0, 3).reshape(LAYERS, 2, width)
    fc1_full = small[:, n_qv : n_qv + n_fc].reshape(n_t, LAYERS, ff_local).transpose(1, 0, 2).reshape(LAYERS, -1)
    table_full = (
        small[:, n_qv + n_fc :].reshape(n_t, LAYERS, heads_local, TABLE).transpose(1, 0, 2, 3).reshape(LAYERS, heads, TABLE)
    ).astype(F32)
    fc1_full = fc1_full.astype(F32)
    qv_full = qv_full.astype(F32)

    pad = SLOT - win_tokens
    index_padded = jnp.pad(rel_index, ((0, pad), (0, pad)), constant_values=-1).reshape(-1)
    one_hot = (index_padded[None, :] == jnp.arange(TABLE, dtype=jnp.int32)[:, None]).astype(F32)
    regions = region_ids.reshape(windows, win_tokens)
    shift_mask = jnp.where(regions[:, :, None] == regions[:, None, :], 0.0, MASKED).astype(F32)

    def padded_mask(mask):
        return jnp.pad(
            jnp.pad(mask, ((0, 0), (0, pad), (0, 0))), ((0, 0), (0, 0), (0, pad)), constant_values=PADDED
        )

    masks = [padded_mask(jnp.zeros_like(shift_mask)), padded_mask(shift_mask)]
    biases = [
        jnp.dot(table_full[l], one_hot, precision=EXACT_PRECISION).reshape(groups, LANES // HD * SLOT, SLOT)
        for l in range(LAYERS)
    ]
    places = [placement(tokens, SHIFT * (l % 2)) for l in range(LAYERS)]
    scale_row = jnp.concatenate([jnp.full((width,), score_scale, F32), jnp.ones((2 * width,), F32)])

    residual = inputs.astype(F32)
    store = []
    for l in range(LAYERS):
        whole, residual = lax.optimization_barrier((wholes[l], residual)) if l else (wholes[l], residual)
        weights[l] = unpack_weights(whole)
        qkv_w, proj_w, fc1_w, fc2_w = weights[l]
        place = places[l]
        normed1, inverse1 = normalize(residual)
        attn_in = (normed1 * norm1_gain[l].astype(F32) + norm1_bias[l].astype(F32)).astype(BF16)
        attn_pad = dot(place, attn_in).astype(BF16)
        qkv_bias = jnp.concatenate([qv_full[l, 0], jnp.zeros((width,), F32), qv_full[l, 1]])
        qkv = ((dot(attn_pad, qkv_w) + qkv_bias) * scale_row).astype(BF16)
        mixture = dot(place, attention_forward(qkv, biases[l], masks[l % 2]), 0, 0).astype(BF16)
        residual_mid = residual + dot(mixture, proj_w, 1, 1) + proj_bias[l].astype(F32)
        normed2, inverse2 = normalize(residual_mid)
        ffn_in = (normed2 * norm2_gain[l].astype(F32) + norm2_bias[l].astype(F32)).astype(BF16)
        activated, slope = gelu_parts(dot(ffn_in, fc1_w) + fc1_full[l])
        hidden = activated.astype(BF16)
        slope = slope.astype(BF16)
        store.append((normed1, inverse1, attn_in, qkv, mixture, normed2, inverse2, ffn_in, slope, hidden))
        residual = residual_mid + dot(hidden, fc2_w, 1, 1) + fc2_bias[l].astype(F32)

    g = cotangent.astype(F32)
    weight_grads = [None] * LAYERS
    small_grads = [None] * LAYERS
    for l in reversed(range(LAYERS)):
        qkv_w, proj_w, fc1_w, fc2_w = weights[l]
        place = places[l]
        normed1, inverse1, attn_in, qkv, mixture, normed2, inverse2, ffn_in, slope, hidden = store[l]
        g_fc2_bias = jnp.sum(g, 0)
        gl = g.astype(BF16)
        dpre = dot(gl, fc2_w) * slope.astype(F32)
        dpl = dpre.astype(BF16)
        g_fc1_bias = jnp.sum(dpre, 0)
        g_fc2 = dot(gl, hidden, 0, 0)
        g_fc1 = dot(ffn_in, dpl, 0, 0)
        dffn = dot(dpl, fc1_w, 1, 1)
        g_n2_gain = jnp.sum(dffn * normed2, 0)
        g_n2_bias = jnp.sum(dffn, 0)
        g_mid = g + norm_back(dffn, normed2, inverse2, norm2_gain[l].astype(F32))
        g_proj_bias = jnp.sum(g_mid, 0)
        gm = g_mid.astype(BF16)
        g_proj = dot(gm, mixture, 0, 0)
        dmix = dot(gm, proj_w).astype(BF16)
        dmix_pad = dot(place, dmix).astype(BF16)
        dqkv_pad, dscores, dbias = attention_backward(qkv, dmix_pad, biases[l], masks[l % 2], score_scale)
        g_table = lax.dot_general(
            dscores.reshape(heads, SLOT * SLOT), one_hot, (((1,), (1,)), ((), ())), precision=EXACT_PRECISION
        )
        dqkv = dot(place, dqkv_pad, 0, 0).astype(BF16)
        g_qkv = dot(attn_in, dqkv, 0, 0)
        dattn = dot(dqkv, qkv_w, 1, 1)
        g_n1_gain = jnp.sum(dattn * normed1, 0)
        g_n1_bias = jnp.sum(dattn, 0)
        g = g_mid + norm_back(dattn, normed1, inverse1, norm1_gain[l].astype(F32))
        dbias_rows = jnp.sum(dbias, 0)
        weight_grads[l] = reduce_shards(pack_grads(g_qkv, g_proj, g_fc1, g_fc2)).astype(F32)
        small_grads[l] = [
            g_n1_gain, g_n1_bias, g_proj_bias, g_n2_gain, g_n2_bias, g_fc2_bias,
            dbias_rows[:width], dbias_rows[2 * width :], g_fc1_bias, g_table.reshape(-1),
        ]

    flat = jnp.concatenate([v for l in range(LAYERS) for v in small_grads[l]])
    total = sum_everywhere(flat).reshape(LAYERS, -1)
    vectors = total[:, : 6 * width].reshape(LAYERS, 6, width)
    at = 6 * width
    qv_total = total[:, at : at + 2 * width].reshape(LAYERS, 2, width)
    qv_total = lax.dynamic_slice_in_dim(qv_total, t_index * local, local, 2)
    at += 2 * width
    fc1_total = lax.dynamic_slice_in_dim(total[:, at : at + ff_local * n_t], t_index * ff_local, ff_local, 1)
    at += ff_local * n_t
    table_total = lax.dynamic_slice_in_dim(
        total[:, at:].reshape(LAYERS, heads, TABLE), t_index * heads_local, heads_local, 1
    )
    grads = jnp.stack(weight_grads)
    qkv_total = grads[..., : cuts[0]].reshape(LAYERS, shard, 3, local).transpose(0, 2, 1, 3)
    proj_w_total = grads[..., cuts[0] : cuts[1]].transpose(0, 2, 1)
    fc1_w_total = grads[..., cuts[1] : cuts[2]]
    fc2_w_total = grads[..., cuts[2] :].transpose(0, 2, 1)
    return (
        residual,
        g,
        vectors[:, 0],
        vectors[:, 1],
        qkv_total,
        qv_total,
        table_total,
        proj_w_total,
        vectors[:, 2],
        vectors[:, 3],
        vectors[:, 4],
        fc1_w_total,
        fc1_total,
        fc2_w_total,
        vectors[:, 5],
    )


def gather_shards(packed):
    n_dp, n_t = lax.axis_size("dp"), lax.axis_size("tensor")
    rows = lax.all_gather(packed, ("dp", "tensor"), axis=0, tiled=False)
    return rows.reshape((n_dp, n_t) + packed.shape)


def reduce_shards(packed):
    rows = packed.reshape((-1,) + packed.shape[2:])
    return lax.psum_scatter(rows, ("dp", "tensor"), scatter_dimension=0, tiled=False)


def partners():
    found = []
    for axis in ("tensor", "dp"):
        size, bit = lax.axis_size(axis), 1
        assert size & (size - 1) == 0
        me = lax.axis_index(axis)
        while bit < size:
            found.append((axis, me + bit - 2 * bit * ((me // bit) % 2)))
            bit *= 2
    return found


def exchange_kernel(x_ref, out_ref, held, arrived, send_sem, recv_sem):
    steps = partners()
    barrier = pltpu.get_barrier_semaphore()
    for axis, place in steps:
        pl.semaphore_signal(barrier, inc=1, device_id={axis: place}, device_id_type=pl.DeviceIdType.MESH)
    pl.semaphore_wait(barrier, len(steps))
    for s, (axis, place) in enumerate(steps):
        source = x_ref if s == 0 else held.at[s - 1]
        copy = pltpu.make_async_remote_copy(
            src_ref=source,
            dst_ref=arrived.at[s],
            send_sem=send_sem.at[s],
            recv_sem=recv_sem.at[s],
            device_id={axis: place},
            device_id_type=pl.DeviceIdType.MESH,
        )
        copy.start()
        copy.wait()
        total = source[...] + arrived[s]
        if s < len(steps) - 1:
            held[s] = total
        else:
            out_ref[...] = total


def sum_everywhere(flat):
    size = flat.shape[0]
    rows = -(-size // (8 * LANES)) * 8
    x = jnp.pad(flat, (0, rows * LANES - size)).reshape(rows, LANES)
    n = len(partners())
    total = pl.pallas_call(
        exchange_kernel,
        out_shape=jax.ShapeDtypeStruct(x.shape, F32),
        in_specs=[pl.BlockSpec(memory_space=pltpu.VMEM)],
        out_specs=pl.BlockSpec(memory_space=pltpu.VMEM),
        scratch_shapes=[
            pltpu.VMEM((n,) + x.shape, F32),
            pltpu.VMEM((n,) + x.shape, F32),
            pltpu.SemaphoreType.DMA((n,)),
            pltpu.SemaphoreType.DMA((n,)),
        ],
        compiler_params=pltpu.CompilerParams(collective_id=0, has_side_effects=True),
        name="sum_everywhere",
    )(x)
    return total.reshape(-1)[:size]


def solution(mesh):
    in_specs = (
        P(("dp", "tensor"), None),
        P(("dp", "tensor"), None),
        P(),
        P(),
        P(),
        P(),
        P(None, None, "dp", "tensor"),
        P(None, None, "tensor"),
        P(None, "tensor", None),
        P(None, "tensor", "dp"),
        P(),
        P(),
        P(),
        P(None, "dp", "tensor"),
        P(None, "tensor"),
        P(None, "tensor", "dp"),
        P(),
    )
    out_specs = (
        P(("dp", "tensor"), None),
        P(("dp", "tensor"), None),
        P(),
        P(),
        P(None, None, "dp", "tensor"),
        P(None, None, "tensor"),
        P(None, "tensor", None),
        P(None, "tensor", "dp"),
        P(),
        P(),
        P(),
        P(None, "dp", "tensor"),
        P(None, "tensor"),
        P(None, "tensor", "dp"),
        P(),
    )
    return jax.shard_map(
        per_device, mesh=mesh, in_specs=in_specs, out_specs=out_specs, check_vma=False
    )
```
